256 devices in a mesh: co: 32 (over y_hi, z, core), ci: 8 (over y_lo, x).
Axes of the slice: x: 4, y: 4 (y_hi: 2, y_lo: 2; y = y_hi * 2 + y_lo), z: 8, core: 2. Of those that a mesh axis runs over, the one named last changes fastest.
Arguments:
- features: bfloat16 [1024, 2048], P('ci'), may hold values from -6 to 6
- filter_bank: bfloat16 [27, 1024, 1024], P(None, 'co', 'ci'), may hold values from -0.0390625 to 0.0390625
- out_grad: bfloat16 [1024, 2048], P('co', 'ci'), may hold values from -6 to 6
Outputs:
- response: bfloat16 [1024, 2048], P('co', 'ci')
- in_grad: bfloat16 [1024, 2048], P('ci', 'co')
- filter_grad: float32 [27, 1024, 1024], P(None, 'co', 'ci')
The draws below stay inside these ranges and needn't reach their ends.
All inputs are finite; a program needn't handle non-finite values.
Results may differ from the reference program's by a relative error of at most 0.001.
Values may be sent and summed in bfloat16 or wider, within the bound.
No kernel may reach another device: no remote copies, remote signals or barrier semaphores. Data moves between devices by JAX's collectives and lax.ppermute only.
A program may use at most 64 MiB of HBM per device.

```python
import jax
import jax.numpy as jnp
from jax import lax

CIN = 1024
COUT = 1024
NY = 8
NZ = 8
NX = 32
TAPS = 27


def with_spikes(drawn, stream_key, source, target, blocks, factor):
    owner, partner = [(jnp.arange(drawn.shape[dim]) // (drawn.shape[dim] // blocks)).reshape([-1 if axis == dim else 1 for axis in range(drawn.ndim)]) for dim in (source, target)]
    chosen = jax.random.permutation(stream_key, blocks)[partner]
    strong = (owner == chosen) | (owner == (partner + blocks // 2) % blocks)
    return jnp.where(strong, factor * drawn, drawn)


def level_of(own_key, dims, split, smallest, top_value):
    def one(axis_at, parts):
        heights = jax.random.uniform(jax.random.fold_in(jax.random.fold_in(own_key, 6), axis_at), (parts,), jnp.float32, smallest / len(split), top_value / len(split))
        return jnp.repeat(jnp.exp(heights), dims[axis_at] // parts).reshape((-1,) + (1,) * (len(dims) - axis_at - 1))

    loudness = one(*split[0])
    for cut in split[1:]:
        loudness = loudness * one(*cut)
    return loudness


def noise(rng, dims, spread, bound, cuts=(), dtype=jnp.bfloat16):
    factor_of = level_of(rng, dims, cuts, -0.22, 0.18) if cuts else 1.0
    entries = jax.random.normal(rng, dims, jnp.float32) * spread * factor_of
    return jnp.minimum(jnp.maximum(entries, -bound), bound).astype(dtype)


def noise_with(key, extent, deviation, bound, cuts, heavy, held_as=jnp.bfloat16):
    drawn = deviation * jax.random.normal(key, extent, jnp.float32)
    if cuts:
        drawn = drawn * level_of(key, extent, cuts, -0.22, 0.18)
    return jnp.clip(with_spikes(drawn, jax.random.fold_in(key, 3), *heavy), -bound, bound).astype(held_as)


def setup_inputs(seed: int = 0) -> dict:
    keys = jax.random.split(jax.random.key(seed), 4)
    features = noise_with(keys[0], (CIN, NX * NY * NZ), 1.0, 6.0, ((0, 8),), (0, 1, 8, 2.0))
    filter_bank = noise(keys[1], (TAPS, COUT, CIN), (TAPS * CIN) ** -0.5, 0.0390625, ((1, 32), (2, 8)))
    out_grad = noise_with(keys[2], (COUT, NX * NY * NZ), 1.0, 6.0, ((0, 32), (1, 8)), (0, 1, 32, 2.75))
    return {"features": features, "filter_bank": filter_bank, "out_grad": out_grad}


def reference(features, filter_bank, out_grad):
    cell_count = NX * NY * NZ
    volume = features.astype(jnp.float32).reshape(1, CIN, NX, NY, NZ)
    kernel = filter_bank.astype(jnp.float32).reshape(3, 3, 3, COUT, CIN)
    pads = ((1, 1), (1, 1), (1, 1))
    response = lax.conv_general_dilated(volume, kernel, (1, 1, 1), pads, dimension_numbers=("NCDHW", "DHWOI", "NCDHW"), precision=lax.Precision.HIGHEST)
    response = response.reshape(COUT, cell_count).astype(jnp.bfloat16)
    gradient = out_grad.astype(jnp.float32)
    flipped = kernel[::-1, ::-1, ::-1]
    in_grad = lax.conv_general_dilated(gradient.reshape(1, COUT, NX, NY, NZ), flipped, (1, 1, 1), pads, dimension_numbers=("NCDHW", "DHWIO", "NCDHW"), precision=lax.Precision.HIGHEST)
    in_grad = in_grad.reshape(CIN, cell_count).astype(jnp.bfloat16)
    padded = jnp.pad(features.astype(jnp.float32).reshape(CIN, NX, NY, NZ), ((0, 0), (1, 1), (1, 1), (1, 1)))
    scale = float(cell_count) ** -0.5
    blocks = []
    for first in range(3):
        for second in range(3):
            for third in range(3):
                shifted = padded[:, first:first + NX, second:second + NY, third:third + NZ].reshape(CIN, cell_count)
                blocks.append(jnp.dot(gradient, shifted.T, precision=lax.Precision.HIGHEST) * scale)
    filter_grad = jnp.stack(blocks, axis=0)
    return response, in_grad, filter_grad
```

```python
import jax
import jax.numpy as jnp
from jax import lax
from jax.sharding import PartitionSpec as P

NY = 8
NZ = 8


def body(features, filter_bank, out_grad):
    chan_in, cell_count = features.shape
    chan_out = filter_bank.shape[1]
    planes = cell_count // (NY * NZ)
    n_ci = lax.axis_size("ci")
    n_co = lax.axis_size("co")
    pads = ((1, 1), (1, 1), (1, 1))
    pieces = jnp.broadcast_to(out_grad[None], (n_ci,) + out_grad.shape)
    pieces = lax.all_to_all(pieces, "ci", 0, 0, tiled=True)
    grad_full = pieces.transpose(1, 0, 2).reshape(chan_out, cell_count)

    volume = features.reshape(1, chan_in, planes, NY, NZ)
    kernel = filter_bank.reshape(3, 3, 3, chan_out, chan_in)
    partial_value = lax.conv_general_dilated(
        volume,
        kernel,
        (1, 1, 1),
        pads,
        dimension_numbers=("NCDHW", "DHWOI", "NCDHW"),
        preferred_element_type=jnp.float32,
    )
    partial_value = partial_value.reshape(chan_out, n_ci, cell_count // n_ci).transpose(1, 0, 2)
    terms = lax.all_to_all(partial_value, "ci", 0, 0, tiled=True)
    response = jnp.sum(terms, axis=0).astype(jnp.bfloat16)

    flipped = kernel[::-1, ::-1, ::-1]
    grad_terms = lax.conv_general_dilated(
        grad_full.reshape(1, chan_out, planes, NY, NZ),
        flipped,
        (1, 1, 1),
        pads,
        dimension_numbers=("NCDHW", "DHWIO", "NCDHW"),
        preferred_element_type=jnp.float32,
    )
    grad_terms = grad_terms.reshape(chan_in, n_co // 2, 2, cell_count // n_co).transpose(1, 2, 3, 0)
    pairs = [[2 * i, 2 * i + 1] for i in range(n_co // 2)]
    same = [[2 * i + c for i in range(n_co // 2)] for c in range(2)]
    halves = lax.all_to_all(grad_terms, "co", 1, 1, tiled=True, axis_index_groups=pairs)
    halves = jnp.sum(halves, axis=1)
    shares = lax.all_to_all(halves, "co", 0, 0, tiled=True, axis_index_groups=same)
    in_grad = jnp.sum(shares, axis=0).T.astype(jnp.bfloat16)

    weight_terms = lax.conv_general_dilated(
        features.reshape(chan_in, 1, planes, NY, NZ),
        grad_full.reshape(chan_out, 1, planes, NY, NZ),
        (1, 1, 1),
        pads,
        dimension_numbers=("NCDHW", "OIDHW", "NCDHW"),
        preferred_element_type=jnp.float32,
    )
    scale = float(cell_count) ** (-0.5)
    filter_grad = (weight_terms * scale).transpose(2, 3, 4, 1, 0).reshape(27, chan_out, chan_in)
    return (response, in_grad, filter_grad)


def solution(mesh):
    placed = (P("ci", None), P(None, "co", "ci"), P("co", "ci"))
    return jax.shard_map(
        body,
        mesh=mesh,
        in_specs=placed,
        out_specs=(P("co", "ci"), P("ci", "co"), P(None, "co", "ci")),
        check_vma=False,
    )
```

```python
import jax
import jax.numpy as jnp
from jax import lax
from jax.experimental import pallas as pl
from jax.experimental.pallas import tpu as pltpu
from jax.sharding import PartitionSpec as P

NY = 8
NZ = 8
AREA = NY * NZ
LANES = 128
F32 = jnp.float32
BF16 = jnp.bfloat16


VMEM = pltpu.VMEM
SHIFTS = [(b, c) for b in (-1, 0, 1) for c in (-1, 0, 1)]


def in_vmem(n):
    return [pl.BlockSpec(memory_space=VMEM)] * n


def shift_rows(value, b, c):
    rows, lanes = value.shape
    if c:
        z = lax.broadcasted_iota(jnp.int32, value.shape, 0) % NZ
        rolled = pltpu.roll(value, (-c) % rows, 0)
        value = jnp.where(z == (NZ - 1 if c > 0 else 0), 0.0, rolled)
    if b:
        cube = value.reshape(rows // AREA, NY, NZ, lanes)
        edge = jnp.zeros((rows // AREA, 1, NZ, lanes), value.dtype)
        if b > 0:
            cube = jnp.concatenate([cube[:, 1:], edge], axis=1)
        else:
            cube = jnp.concatenate([edge, cube[:, :-1]], axis=1)
        value = cube.reshape(rows, lanes)
    return value


def pack_kernel(grad_ref, out_ref):
    tiles = []
    for t in range(2):
        tile = grad_ref[:, t * LANES:(t + 1) * LANES].astype(F32)
        tiles += [tile, pltpu.roll(tile, AREA, 1)]
    packed = jnp.concatenate(tiles, axis=0).T[:AREA].astype(BF16)
    for r in range(out_ref.shape[0]):
        out_ref[r] = packed


def response_kernel(x_ref, f_ref, out_ref, wide_ref, lhs, rhs):
    groups = out_ref.shape[0]
    planes = 4 * groups
    width = 6 * LANES
    zero = jnp.zeros((AREA, LANES), BF16)
    for s in range(9):
        lhs[0:AREA, s * width:s * width + LANES] = zero
        lhs[(groups - 1) * AREA:groups * AREA, (s + 1) * width - LANES:(s + 1) * width] = zero
        for i in range(4):
            for j in range(6):
                a = j - 1 - i
                block = f_ref[(a + 1) * 9 + s] if -1 <= a <= 1 else jnp.zeros((32, LANES), BF16)
                rhs[i * 32:(i + 1) * 32, s * width + j * LANES:s * width + (j + 1) * LANES] = block
    for pair in range(planes // 2):
        cells = x_ref[:, pair * LANES:(pair + 1) * LANES].astype(F32).T
        by_z = [shift_rows(cells, 0, c) for c in (-1, 0, 1)]
        for s, (b, c) in enumerate(SHIFTS):
            moved = shift_rows(by_z[c + 1], b, 0).astype(BF16)
            for half in range(2):
                plane = 2 * pair + half
                piece = moved[half * AREA:(half + 1) * AREA]
                group, i = plane // 4, plane % 4
                spots = [(group, i + 1)]
                if i == 3 and group + 1 < groups:
                    spots.append((group + 1, 0))
                if i == 0 and group:
                    spots.append((group - 1, 5))
                for g, j in spots:
                    lhs[g * AREA:(g + 1) * AREA, s * width + j * LANES:s * width + (j + 1) * LANES] = piece
    wide_ref[...] = lhs[:, 4 * width:5 * width]
    total = lax.dot_general(lhs[...], rhs[...], (((1,), (1,)), ((), ())), preferred_element_type=F32)
    out_ref[...] = total.reshape(out_ref.shape)


def in_grad_kernel(place_ref, mine_ref, other_ref, f0_ref, f1_ref, f2_ref, f3_ref, out_ref, lhs, rhs):
    groups = out_ref.shape[0]
    zpar = place_ref[0]
    q = place_ref[1]
    rows = groups * AREA
    filters = (f0_ref, f1_ref, f2_ref, f3_ref)
    lane = lax.broadcasted_iota(jnp.int32, (rows, LANES), 1)
    own_lane = jnp.where(q == 0, jnp.where(lane >= 32, 1, 0), jnp.where(lane < 160 - 32 * q, 1, 0)) == 1
    back = lax.rem(jnp.int32(160) - 32 * q, jnp.int32(LANES))
    edge = jnp.zeros((AREA, LANES), F32)
    for source in range(4):
        ref = mine_ref if source < 2 else other_ref
        sel = zpar if source % 2 == 0 else 1 - zpar
        block = ref[sel].reshape(rows, LANES).astype(F32)
        rolled = pltpu.roll(block, back, 1)
        below = jnp.concatenate([edge, rolled[:-AREA]], axis=0)
        above = jnp.concatenate([rolled[AREA:], edge], axis=0)
        near = jnp.where(own_lane, rolled, jnp.where(q == 0, below, above))
        by_z = [shift_rows(near, 0, -c) for c in (-1, 0, 1)]
        for s, (b, c) in enumerate(SHIFTS):
            at = (s * 4 + source) * LANES
            lhs[:, at:at + LANES] = shift_rows(by_z[c + 1], -b, 0).astype(BF16)
            for j in range(3):
                rhs[at + j * 32:at + (j + 1) * 32, :] = filters[source][(2 - j) * 9 + s]
            rhs[at + 96:at + LANES, :] = jnp.zeros((32, LANES), BF16)
    total = jnp.dot(lhs[...], rhs[...], preferred_element_type=F32)
    out_ref[...] = total.reshape(out_ref.shape)


def filter_grad_kernel(place_ref, mine_ref, wide_ref, out_ref, *, scale):
    groups = mine_ref.shape[1]
    block = mine_ref[place_ref[0]].astype(F32).reshape(groups * AREA, LANES)
    turned = jnp.concatenate([block[k * LANES:(k + 1) * LANES].T for k in range(groups * AREA // LANES)], axis=1)
    cells = turned.shape[1]
    index = lax.broadcasted_iota(jnp.int32, turned.shape, 1)
    z = index % NZ
    y = (index // NZ) % NY
    wide = wide_ref[...]
    for s, (b, c) in enumerate(SHIFTS):
        moved = turned
        step = b * NZ + c
        if step:
            moved = pltpu.roll(turned, step % cells, 1)
        if c:
            moved = jnp.where(z == (0 if c > 0 else NZ - 1), 0.0, moved)
        if b:
            moved = jnp.where(y == (0 if b > 0 else NY - 1), 0.0, moved)
        full = jnp.dot(moved.astype(BF16), wide, preferred_element_type=F32)
        for a in (-1, 0, 1):
            total = None
            for i in range(4):
                j = i + a + 1
                part = full[i * 32:(i + 1) * 32, j * LANES:(j + 1) * LANES]
                total = part if total is None else total + part
            out_ref[(a + 1) * 9 + s] = total * scale


def pack(out_grad, receivers):
    return pl.pallas_call(
        pack_kernel,
        out_shape=jax.ShapeDtypeStruct((receivers, AREA, LANES), BF16),
        in_specs=in_vmem(1),
        out_specs=in_vmem(1)[0],
        name="pack",
    )(out_grad)


def response_terms(features, bank):
    groups = features.shape[1] // (4 * AREA)
    rows = groups * AREA
    return pl.pallas_call(
        response_kernel,
        out_shape=(
            jax.ShapeDtypeStruct((groups, AREA, LANES), F32),
            jax.ShapeDtypeStruct((rows, 6 * LANES), BF16),
        ),
        in_specs=in_vmem(2),
        out_specs=tuple(in_vmem(2)),
        scratch_shapes=[VMEM((rows, 54 * LANES), BF16), VMEM((LANES, 54 * LANES), BF16)],
        name="response_terms",
    )(features, bank)


def in_grad_terms(place, mine, other, banks):
    groups = mine.shape[1]
    rows = groups * AREA
    return pl.pallas_call(
        in_grad_kernel,
        out_shape=jax.ShapeDtypeStruct((groups, AREA, LANES), F32),
        in_specs=[pl.BlockSpec(memory_space=pltpu.SMEM)] + in_vmem(6),
        out_specs=in_vmem(1)[0],
        scratch_shapes=[VMEM((rows, 36 * LANES), BF16), VMEM((36 * LANES, LANES), BF16)],
        name="in_grad_terms",
    )(place, mine, other, *banks)


def filter_terms(place, mine, wide, scale):
    return pl.pallas_call(
        lambda *refs: filter_grad_kernel(*refs, scale=scale),
        out_shape=jax.ShapeDtypeStruct((27, 32, LANES), F32),
        in_specs=[pl.BlockSpec(memory_space=pltpu.SMEM)] + in_vmem(2),
        out_specs=in_vmem(1)[0],
        name="filter_terms",
    )(place, mine, wide)


def body(features, bank, out_grad):
    cell_count = features.shape[1]
    n_ci = lax.axis_size("ci")
    n_co = lax.axis_size("co")
    co = lax.axis_index("co")
    place = jnp.stack([(co // 2) % 2, co % 4]).astype(jnp.int32)

    other_z = [(i, i ^ 2) for i in range(n_co)]
    other_core = [(i, i ^ 1) for i in range(n_co)]
    gather_groups = [
        [(4 * k + 2 * h + c) * n_ci + i for h in range(2) for i in range(n_ci)]
        for k in range(n_co // 4)
        for c in range(2)
    ]
    sum_groups = [[4 * k + q for k in range(n_co // 4)] for q in range(4)]

    bank_z = lax.ppermute(bank, "co", other_z)
    packed = pack(out_grad, 2 * n_ci)
    mine = lax.all_to_all(packed, ("co", "ci"), 0, 0, tiled=True, axis_index_groups=gather_groups)
    mine = mine.reshape(2, n_ci, AREA, LANES)
    terms, wide = response_terms(features, bank)
    bank_c = lax.ppermute(bank, "co", other_core)
    bank_cz = lax.ppermute(bank_z, "co", other_core)
    other = lax.ppermute(mine, "co", other_core)

    shares = in_grad_terms(place, mine, other, (bank, bank_z, bank_c, bank_cz))
    shares = lax.all_to_all(shares, "co", 0, 0, tiled=True, axis_index_groups=sum_groups)
    in_grad = jnp.sum(shares, axis=0).T.astype(BF16)

    terms = lax.all_to_all(terms, "ci", 0, 0, tiled=True)
    response = jnp.sum(terms, axis=0).reshape(AREA, 4, 32).transpose(2, 1, 0)
    response = response.reshape(32, 4 * AREA).astype(BF16)

    filter_grad = filter_terms(place, mine, wide, float(cell_count) ** (-0.5))
    return (response, in_grad, filter_grad)


def solution(mesh):
    placed = (P("ci", None), P(None, "co", "ci"), P("co", "ci"))
    return jax.shard_map(
        body,
        mesh=mesh,
        in_specs=placed,
        out_specs=(P("co", "ci"), P("ci", "co"), P(None, "co", "ci")),
        check_vma=False,
    )
```

```python
import jax
import jax.numpy as jnp
from jax import lax
from jax.experimental import pallas as pl
from jax.experimental.pallas import tpu as pltpu
from jax.sharding import PartitionSpec as P


NY = 8
NZ = 8
AREA = NY * NZ
LANES = 128
F32 = jnp.float32
BF16 = jnp.bfloat16


VMEM = pltpu.VMEM
SHIFTS = [(b, c) for b in (-1, 0, 1) for c in (-1, 0, 1)]


def in_vmem(n):
    return [pl.BlockSpec(memory_space=VMEM)] * n


def shift_rows(value, b, c):
    rows, lanes = value.shape
    if c:
        z = lax.broadcasted_iota(jnp.int32, value.shape, 0) % NZ
        rolled = pltpu.roll(value, (-c) % rows, 0)
        value = jnp.where(z == (NZ - 1 if c > 0 else 0), 0.0, rolled)
    if b:
        cube = value.reshape(rows // AREA, NY, NZ, lanes)
        edge = jnp.zeros((rows // AREA, 1, NZ, lanes), value.dtype)
        if b > 0:
            cube = jnp.concatenate([cube[:, 1:], edge], axis=1)
        else:
            cube = jnp.concatenate([edge, cube[:, :-1]], axis=1)
        value = cube.reshape(rows, lanes)
    return value


def position():
    co = lax.axis_index("co")
    return lax.rem(co, 2), lax.rem(co // 2, 2)


def pack_kernel(grad_ref, out_ref):
    tiles = []
    for t in range(2):
        tile = grad_ref[:, t * LANES:(t + 1) * LANES].astype(F32)
        tiles += [tile, pltpu.roll(tile, AREA, 1)]
    packed = jnp.concatenate(tiles, axis=0).T[:AREA].astype(BF16)
    for r in range(out_ref.shape[0]):
        out_ref[r] = packed


def response_kernel(x_ref, f_ref, out_ref, wide_ref, lhs, rhs):
    groups = out_ref.shape[0]
    planes = 4 * groups
    rows = groups * AREA
    width = 4 * LANES
    zero = jnp.zeros((AREA, LANES), BF16)
    rhs[192:, :] = jnp.zeros((AREA, 3 * width), BF16)
    for b in range(3):
        lhs[0:AREA, b * width:b * width + LANES] = zero
        lhs[2 * rows - AREA:2 * rows, (b + 1) * width - LANES:(b + 1) * width] = zero
        for c in range(3):
            for i in range(2):
                for j in range(4):
                    a = j - 1 - i
                    block = f_ref[(a + 1) * 9 + b * 3 + c] if -1 <= a <= 1 else jnp.zeros((32, LANES), BF16)
                    rhs[c * 64 + i * 32:c * 64 + (i + 1) * 32, b * width + j * LANES:b * width + (j + 1) * LANES] = block
    for pair in range(planes // 2):
        cells = x_ref[:, pair * LANES:(pair + 1) * LANES].astype(F32).T
        for b in range(3):
            moved = shift_rows(cells, b - 1, 0).astype(BF16)
            for i in range(2):
                piece = moved[i * AREA:(i + 1) * AREA]
                spots = [(pair, i + 1)]
                if i == 1 and pair + 1 < planes // 2:
                    spots.append((pair + 1, 0))
                if i == 0 and pair:
                    spots.append((pair - 1, 3))
                for p, j in spots:
                    at = (p % 2) * rows + (p // 2) * AREA
                    lhs[at:at + AREA, b * width + j * LANES:b * width + (j + 1) * LANES] = piece
    wide_ref[...] = lhs[:, width:2 * width]
    lane = lax.broadcasted_iota(jnp.int32, (rows, LANES), 1)
    parts = []
    for half in range(2):
        full = lax.dot_general(
            lhs[half * rows:(half + 1) * rows, :], rhs[...], (((1,), (1,)), ((), ())), preferred_element_type=F32
        )
        first = full[:, :LANES]
        last = full[:, LANES:]
        sides = shift_rows(first, 0, -1) + shift_rows(last, 0, 1)
        parts.append((sides, first))
    low = parts[0][0] + pltpu.roll(parts[0][1], AREA, 1)
    high = pltpu.roll(parts[1][0], AREA, 1) + parts[1][1]
    total = jnp.where(lane < AREA, low, high)
    core, _ = position()
    for g in range(groups):
        out_ref[lax.rem(g + core * (groups // 2), groups)] = total[g * AREA:(g + 1) * AREA]


def in_grad_kernel(mine_ref, other_ref, f0_ref, f1_ref, f2_ref, f3_ref, out_ref, lhs, rhs):
    groups = out_ref.shape[0]
    core, zpar = position()
    q = 2 * zpar + core
    rows = groups * AREA
    filters = (f0_ref, f1_ref, f2_ref, f3_ref)
    lane = lax.broadcasted_iota(jnp.int32, (rows, LANES), 1)
    own_lane = jnp.where(q == 0, jnp.where(lane >= 32, 1, 0), jnp.where(lane < 160 - 32 * q, 1, 0)) == 1
    back = lax.rem(160 - 32 * q, LANES)
    edge = jnp.zeros((AREA, LANES), F32)
    for source in range(4):
        ref = mine_ref if source < 2 else other_ref
        sel = lax.rem(zpar + core + source // 2 + source % 2, 2)
        block = ref[sel].reshape(rows, LANES).astype(F32)
        rolled = pltpu.roll(block, back, 1)
        below = jnp.concatenate([edge, rolled[:-AREA]], axis=0)
        above = jnp.concatenate([rolled[AREA:], edge], axis=0)
        near = jnp.where(own_lane, rolled, jnp.where(q == 0, below, above))
        for b in range(3):
            at = (b * 4 + source) * LANES
            lhs[:, at:at + LANES] = shift_rows(near, 1 - b, 0).astype(BF16)
            for c in range(3):
                for j in range(3):
                    rhs[at + j * 32:at + (j + 1) * 32, c * LANES:(c + 1) * LANES] = filters[source][(2 - j) * 9 + b * 3 + c]
                rhs[at + 96:at + LANES, c * LANES:(c + 1) * LANES] = jnp.zeros((32, LANES), BF16)
    full = jnp.dot(lhs[...], rhs[...], preferred_element_type=F32)
    total = shift_rows(full[:, :LANES], 0, 1) + full[:, LANES:2 * LANES] + shift_rows(full[:, 2 * LANES:], 0, -1)
    for k in range(groups):
        out_ref[lax.rem(k + (groups // 4) * q, groups)] = total[k * AREA:(k + 1) * AREA]


def filter_grad_kernel(mine_ref, wide_ref, out_ref, *, scale):
    groups = mine_ref.shape[1]
    rows = groups * AREA
    core, zpar = position()
    block = mine_ref[lax.rem(zpar + core, 2)].astype(F32).reshape(rows, LANES)
    turned = jnp.concatenate([block[k * LANES:(k + 1) * LANES].T for k in range(rows // LANES)], axis=1)
    turned = jnp.concatenate([turned[:64], turned[64:]], axis=1)
    cells = turned.shape[1]
    index = lax.broadcasted_iota(jnp.int32, turned.shape, 1)
    z = index % NZ
    y = (index // NZ) % NY
    wide = wide_ref[...]
    for s, (b, c) in enumerate(SHIFTS):
        moved = turned
        step = b * NZ + c
        if step:
            moved = pltpu.roll(turned, step % cells, 1)
        if c:
            moved = jnp.where(z == (0 if c > 0 else NZ - 1), 0.0, moved)
        if b:
            moved = jnp.where(y == (0 if b > 0 else NY - 1), 0.0, moved)
        full = jnp.dot(moved.astype(BF16), wide, preferred_element_type=F32)
        for a in (-1, 0, 1):
            total = full[:32, (a + 1) * LANES:(a + 2) * LANES] + full[32:, (a + 2) * LANES:(a + 3) * LANES]
            out_ref[(a + 1) * 9 + s] = total * scale


LIMIT = 20 * 2**20


def params():
    return pltpu.CompilerParams(vmem_limit_bytes=LIMIT)


def cost(flops, moved):
    return pl.CostEstimate(flops=flops, transcendentals=0, bytes_accessed=moved)


def pack(out_grad, receivers):
    return pl.pallas_call(
        pack_kernel,
        out_shape=jax.ShapeDtypeStruct((receivers, AREA, LANES), BF16),
        in_specs=in_vmem(1),
        out_specs=in_vmem(1)[0],
        compiler_params=params(),
        name="pack",
    )(out_grad)


def response_terms(features, bank):
    groups = features.shape[1] // (4 * AREA)
    rows = groups * AREA
    return pl.pallas_call(
        response_kernel,
        out_shape=(
            jax.ShapeDtypeStruct((groups, AREA, LANES), F32),
            jax.ShapeDtypeStruct((2 * rows, 4 * LANES), BF16),
        ),
        in_specs=in_vmem(2),
        out_specs=tuple(in_vmem(2)),
        scratch_shapes=[VMEM((2 * rows, 12 * LANES), BF16), VMEM((2 * LANES, 12 * LANES), BF16)],
        compiler_params=params(),
        cost_estimate=cost(2 * 27 * 32 * 128 * 2048, 2 * 10**6),
        name="response_terms",
    )(features, bank)


def in_grad_terms(mine, other, banks):
    groups = mine.shape[1]
    rows = groups * AREA
    return pl.pallas_call(
        in_grad_kernel,
        out_shape=jax.ShapeDtypeStruct((groups, AREA, LANES), F32),
        in_specs=in_vmem(6),
        out_specs=in_vmem(1)[0],
        scratch_shapes=[VMEM((rows, 12 * LANES), BF16), VMEM((12 * LANES, 3 * LANES), BF16)],
        compiler_params=params(),
        cost_estimate=cost(2 * 27 * 32 * 128 * 2048, 2 * 10**6),
        name="in_grad_terms",
    )(mine, other, *banks)


def filter_terms(mine, wide, scale):
    return pl.pallas_call(
        lambda *refs: filter_grad_kernel(*refs, scale=scale),
        out_shape=jax.ShapeDtypeStruct((27, 32, LANES), F32),
        in_specs=in_vmem(2),
        out_specs=in_vmem(1)[0],
        compiler_params=params(),
        cost_estimate=cost(2 * 27 * 32 * 128 * 2048, 2 * 10**6),
        name="filter_terms",
    )(mine, wide)


def body(features, bank, out_grad):
    cell_count = features.shape[1]
    n_ci = lax.axis_size("ci")
    n_co = lax.axis_size("co")
    other_z = [(i, i ^ 2) for i in range(n_co)]
    other_core = [(i, i ^ 1) for i in range(n_co)]
    gather_groups = [
        [(4 * k + 2 * ((h + c) % 2) + c) * n_ci + i for h in range(2) for i in range(n_ci)]
        for k in range(n_co // 4)
        for c in range(2)
    ]
    quads = n_co // 4
    sum_groups = [[4 * ((k - quads // 4 * q) % quads) + q for k in range(quads)] for q in range(4)]
    response_groups = [[o * n_ci + (i - o % 2 * n_ci // 2) % n_ci for i in range(n_ci)] for o in range(n_co)]
    packed = pack(out_grad, 2 * n_ci)
    mine = lax.all_to_all(packed, ("co", "ci"), 0, 0, tiled=True, axis_index_groups=gather_groups)
    mine = mine.reshape(2, n_ci, AREA, LANES)
    bank_z = lax.ppermute(bank, "co", other_z)
    bank_c = lax.ppermute(bank, "co", other_core)
    bank_cz = lax.ppermute(bank_z, "co", other_core)
    terms, wide = response_terms(features, bank)
    other = lax.ppermute(mine, "co", other_core)
    shares = in_grad_terms(mine, other, (bank, bank_z, bank_c, bank_cz))
    shares = lax.all_to_all(shares, "co", 0, 0, tiled=True, axis_index_groups=sum_groups)
    in_grad = jnp.sum(shares, axis=0).T.astype(BF16)
    terms = lax.all_to_all(terms, ("co", "ci"), 0, 0, tiled=True, axis_index_groups=response_groups)
    response = jnp.sum(terms, axis=0).reshape(AREA, 4, 32).transpose(2, 1, 0)
    response = response.reshape(32, 4 * AREA).astype(BF16)
    filter_grad = filter_terms(mine, wide, float(cell_count) ** (-0.5))
    return (response, in_grad, filter_grad)


def solution(mesh):
    placed = (P("ci", None), P(None, "co", "ci"), P("co", "ci"))
    return jax.shard_map(
        body,
        mesh=mesh,
        in_specs=placed,
        out_specs=(P("co", "ci"), P("ci", "co"), P(None, "co", "ci")),
        check_vma=False,
    )
```

```python
import jax
import jax.numpy as jnp
from jax import lax
from jax.experimental import pallas as pl
from jax.experimental.pallas import tpu as pltpu
from jax.sharding import PartitionSpec as P


NY = 8
NZ = 8
AREA = NY * NZ
LANES = 128
F32 = jnp.float32
BF16 = jnp.bfloat16


VMEM = pltpu.VMEM
SHIFTS = [(b, c) for b in (-1, 0, 1) for c in (-1, 0, 1)]


def in_vmem(n):
    return [pl.BlockSpec(memory_space=VMEM)] * n


def shift_rows(value, b, c):
    rows, lanes = value.shape
    if c:
        z = lax.broadcasted_iota(jnp.int32, value.shape, 0) % NZ
        rolled = pltpu.roll(value, (-c) % rows, 0)
        value = jnp.where(z == (NZ - 1 if c > 0 else 0), 0.0, rolled)
    if b:
        cube = value.reshape(rows // AREA, NY, NZ, lanes)
        edge = jnp.zeros((rows // AREA, 1, NZ, lanes), value.dtype)
        if b > 0:
            cube = jnp.concatenate([cube[:, 1:], edge], axis=1)
        else:
            cube = jnp.concatenate([edge, cube[:, :-1]], axis=1)
        value = cube.reshape(rows, lanes)
    return value


def position():
    co = lax.axis_index("co")
    return lax.rem(co, 2), co // (lax.axis_size("co") // 2)


def receiver():
    return lax.axis_index("ci")


def pack_kernel(grad_ref, out_ref):
    tiles = []
    for t in range(2):
        tile = grad_ref[:, t * LANES:(t + 1) * LANES].astype(F32)
        tiles += [tile, pltpu.roll(tile, AREA, 1)]
    packed = jnp.concatenate(tiles, axis=0).T[:AREA].astype(BF16)
    for r in range(out_ref.shape[0]):
        out_ref[r] = packed


def response_kernel(x_ref, f_ref, keep_ref, send_ref, wide_ref, lhs, rhs):
    groups = 2 * keep_ref.shape[0]
    planes = 4 * groups
    rows = groups * AREA
    width = 4 * LANES
    zero = jnp.zeros((AREA, LANES), BF16)
    rhs[192:, :] = jnp.zeros((AREA, 3 * width), BF16)
    for b in range(3):
        lhs[0:AREA, b * width:b * width + LANES] = zero
        lhs[2 * rows - AREA:2 * rows, (b + 1) * width - LANES:(b + 1) * width] = zero
        for c in range(3):
            for i in range(2):
                for j in range(4):
                    a = j - 1 - i
                    block = f_ref[(a + 1) * 9 + b * 3 + c] if -1 <= a <= 1 else jnp.zeros((32, LANES), BF16)
                    rhs[c * 64 + i * 32:c * 64 + (i + 1) * 32, b * width + j * LANES:b * width + (j + 1) * LANES] = block
    for pair in range(planes // 2):
        cells = x_ref[:, pair * LANES:(pair + 1) * LANES].astype(F32).T
        for b in range(3):
            moved = shift_rows(cells, b - 1, 0).astype(BF16)
            for i in range(2):
                piece = moved[i * AREA:(i + 1) * AREA]
                spots = [(pair, i + 1)]
                if i == 1 and pair + 1 < planes // 2:
                    spots.append((pair + 1, 0))
                if i == 0 and pair:
                    spots.append((pair - 1, 3))
                for p, j in spots:
                    at = (p % 2) * rows + (p // 2) * AREA
                    lhs[at:at + AREA, b * width + j * LANES:b * width + (j + 1) * LANES] = piece
    wide_ref[...] = lhs[:, width:2 * width]
    lane = lax.broadcasted_iota(jnp.int32, (rows, LANES), 1)
    parts = []
    for half in range(2):
        full = lax.dot_general(
            lhs[half * rows:(half + 1) * rows, :], rhs[...], (((1,), (1,)), ((), ())), preferred_element_type=F32
        )
        first = full[:, :LANES]
        last = full[:, LANES:]
        sides = shift_rows(first, 0, -1) + shift_rows(last, 0, 1)
        parts.append((sides, first))
    low = parts[0][0] + pltpu.roll(parts[0][1], AREA, 1)
    high = pltpu.roll(parts[1][0], AREA, 1) + parts[1][1]
    total = jnp.where(lane < AREA, low, high)
    mask = lax.bitwise_and(receiver(), groups // 2 - 1)
    lower = receiver() < groups // 2
    for g in range(groups // 2):
        near = total[g * AREA:(g + 1) * AREA]
        far = total[(g + groups // 2) * AREA:(g + groups // 2 + 1) * AREA]
        at = lax.bitwise_xor(mask, g)
        keep_ref[at] = jnp.where(lower, near, far)
        send_ref[at] = jnp.where(lower, far, near)


def add_kernel(mine_ref, other_ref, keep_ref, send_ref):
    for p in range(mine_ref.shape[0]):
        total = mine_ref[p] + other_ref[p]
        if p % 2:
            send_ref[p // 2] = total
        else:
            keep_ref[p // 2] = total


def response_out_kernel(mine_ref, other_ref, out_ref):
    total = mine_ref[0] + other_ref[0]
    turned = jnp.concatenate([total, total], axis=0).T
    lane = lax.broadcasted_iota(jnp.int32, (32, LANES), 1)
    for t in range(2):
        low = turned[t * 64:t * 64 + 32]
        high = turned[t * 64 + 32:t * 64 + 64]
        out_ref[:, t * LANES:(t + 1) * LANES] = jnp.where(lane < AREA, low, high).astype(BF16)


def in_grad_kernel(mine_ref, other_ref, f0_ref, f1_ref, f2_ref, f3_ref, out_ref, lhs, rhs):
    groups = out_ref.shape[0]
    held = groups // 2
    core, half = position()
    filters = (f0_ref, f1_ref, f2_ref, f3_ref)
    lane = lax.broadcasted_iota(jnp.int32, (AREA, LANES), 1)
    for source in range(4):
        ref = mine_ref if source < 2 else other_ref
        sel = half if source % 2 == 0 else 1 - half
        blocks = []
        for m in range(-1, held + 1):
            at = half * held + m
            block = ref[sel, jnp.clip(at, 0, groups - 1)].astype(F32)
            if m in (-1, held):
                block = jnp.where(jnp.logical_and(at >= 0, at < groups), block, 0.0)
            blocks.append(block)
        early = [pltpu.roll(block, 32 * (1 - core), 1) for block in blocks[:-1]]
        late = [pltpu.roll(block, LANES - 32 * (core + 1), 1) for block in blocks[1:]]
        rows = []
        for m in range(held):
            rows.append(jnp.where(lane >= 32 * (1 - core), early[m + 1], early[m]))
            rows.append(jnp.where(lane < LANES - 32 * (core + 1), late[m], late[m + 1]))
        near = jnp.concatenate(rows, axis=0)
        for b in range(3):
            at = (b * 4 + source) * LANES
            lhs[:, at:at + LANES] = shift_rows(near, 1 - b, 0).astype(BF16)
            for c in range(3):
                for j in range(3):
                    rhs[at + j * 32:at + (j + 1) * 32, c * LANES:(c + 1) * LANES] = filters[source][(2 - j) * 9 + b * 3 + c]
                rhs[at + 96:at + LANES, c * LANES:(c + 1) * LANES] = jnp.zeros((32, LANES), BF16)
    full = jnp.dot(lhs[...], rhs[...], preferred_element_type=F32)
    total = shift_rows(full[:, :LANES], 0, 1) + full[:, LANES:2 * LANES] + shift_rows(full[:, 2 * LANES:], 0, -1)
    out_ref[...] = total.reshape(out_ref.shape)


def filter_grad_kernel(mine_ref, wide_ref, out_ref, *, scale):
    groups = mine_ref.shape[1]
    rows = groups * AREA
    block = mine_ref[position()[1]].astype(F32).reshape(rows, LANES)
    turned = jnp.concatenate([block[k * LANES:(k + 1) * LANES].T for k in range(rows // LANES)], axis=1)
    turned = jnp.concatenate([turned[:64], turned[64:]], axis=1)
    cells = turned.shape[1]
    index = lax.broadcasted_iota(jnp.int32, turned.shape, 1)
    z = index % NZ
    y = (index // NZ) % NY
    wide = wide_ref[...]
    for s, (b, c) in enumerate(SHIFTS):
        moved = turned
        step = b * NZ + c
        if step:
            moved = pltpu.roll(turned, step % cells, 1)
        if c:
            moved = jnp.where(z == (0 if c > 0 else NZ - 1), 0.0, moved)
        if b:
            moved = jnp.where(y == (0 if b > 0 else NY - 1), 0.0, moved)
        full = jnp.dot(moved.astype(BF16), wide, preferred_element_type=F32)
        for a in (-1, 0, 1):
            total = full[:32, (a + 1) * LANES:(a + 2) * LANES] + full[32:, (a + 2) * LANES:(a + 3) * LANES]
            out_ref[(a + 1) * 9 + s] = total * scale


LIMIT = 20 * 2**20


def params():
    return pltpu.CompilerParams(vmem_limit_bytes=LIMIT)


def cost(flops, moved):
    return pl.CostEstimate(flops=flops, transcendentals=0, bytes_accessed=moved)


def pack(out_grad, receivers):
    return pl.pallas_call(
        pack_kernel,
        out_shape=jax.ShapeDtypeStruct((receivers, AREA, LANES), BF16),
        in_specs=in_vmem(1),
        out_specs=in_vmem(1)[0],
        compiler_params=params(),
        name="pack",
    )(out_grad)


def response_terms(features, bank):
    groups = features.shape[1] // (4 * AREA)
    rows = groups * AREA
    return pl.pallas_call(
        response_kernel,
        out_shape=(
            jax.ShapeDtypeStruct((groups // 2, AREA, LANES), F32),
            jax.ShapeDtypeStruct((groups // 2, AREA, LANES), F32),
            jax.ShapeDtypeStruct((2 * rows, 4 * LANES), BF16),
        ),
        in_specs=in_vmem(2),
        out_specs=tuple(in_vmem(3)),
        scratch_shapes=[VMEM((2 * rows, 12 * LANES), BF16), VMEM((2 * LANES, 12 * LANES), BF16)],
        compiler_params=params(),
        cost_estimate=cost(2 * 27 * 32 * 128 * 2048, 2 * 10**6),
        name="response_terms",
    )(features, bank)


def add_terms(mine, other):
    part = jax.ShapeDtypeStruct((mine.shape[0] // 2, AREA, LANES), F32)
    return pl.pallas_call(
        add_kernel,
        out_shape=(part, part),
        in_specs=in_vmem(2),
        out_specs=tuple(in_vmem(2)),
        compiler_params=params(),
        name="add_terms",
    )(mine, other)


def response_out(mine, other):
    return pl.pallas_call(
        response_out_kernel,
        out_shape=jax.ShapeDtypeStruct((32, 4 * AREA), BF16),
        in_specs=in_vmem(2),
        out_specs=in_vmem(1)[0],
        compiler_params=params(),
        name="response_out",
    )(mine, other)


def in_grad_terms(mine, other, banks):
    groups = mine.shape[1]
    rows = groups * AREA
    return pl.pallas_call(
        in_grad_kernel,
        out_shape=jax.ShapeDtypeStruct((groups, AREA, LANES), F32),
        in_specs=in_vmem(6),
        out_specs=in_vmem(1)[0],
        scratch_shapes=[VMEM((rows, 12 * LANES), BF16), VMEM((12 * LANES, 3 * LANES), BF16)],
        compiler_params=params(),
        cost_estimate=cost(2 * 27 * 32 * 128 * 2048, 2 * 10**6),
        name="in_grad_terms",
    )(mine, other, *banks)


def filter_terms(mine, wide, scale):
    return pl.pallas_call(
        lambda *refs: filter_grad_kernel(*refs, scale=scale),
        out_shape=jax.ShapeDtypeStruct((27, 32, LANES), F32),
        in_specs=in_vmem(2),
        out_specs=in_vmem(1)[0],
        compiler_params=params(),
        cost_estimate=cost(2 * 27 * 32 * 128 * 2048, 2 * 10**6),
        name="filter_terms",
    )(mine, wide)


def body(features, bank, out_grad):
    cell_count = features.shape[1]
    n_ci = lax.axis_size("ci")
    n_co = lax.axis_size("co")
    column = n_co // 2
    other_y = [(i, (i + column) % n_co) for i in range(n_co)]
    other_core = [(i, i ^ 1) for i in range(n_co)]
    gather_groups = [[(h * column + k) * n_ci + i for h in range(2) for i in range(n_ci)] for k in range(column)]
    sum_groups = [[h * column + 2 * z + c for z in range(column // 2)] for h in range(2) for c in range(2)]
    flips = [[(i, i ^ d) for i in range(n_ci)] for d in (n_ci // 2, 1, 2)]
    packed = pack(out_grad, 2 * n_ci)
    mine = lax.all_to_all(packed, ("co", "ci"), 0, 0, tiled=True, axis_index_groups=gather_groups)
    mine = mine.reshape(2, n_ci, AREA, LANES)
    bank_y = lax.ppermute(bank, "co", other_y)
    bank_c = lax.ppermute(bank, "co", other_core)
    bank_cy = lax.ppermute(bank_y, "co", other_core)
    keep, send, wide = response_terms(features, bank)
    came = lax.ppermute(send, "ci", flips[0])
    keep, send = add_terms(keep, came)
    came = lax.ppermute(send, "ci", flips[1])
    keep, send = add_terms(keep, came)
    came = lax.ppermute(send, "ci", flips[2])
    response = response_out(keep, came)
    other = lax.ppermute(mine, "co", other_core)
    shares = in_grad_terms(mine, other, (bank, bank_y, bank_c, bank_cy))
    shares = lax.all_to_all(shares, "co", 0, 0, tiled=True, axis_index_groups=sum_groups)
    in_grad = jnp.sum(shares, axis=0).T.astype(BF16)
    filter_grad = filter_terms(mine, wide, float(cell_count) ** (-0.5))
    return (response, in_grad, filter_grad)


def solution(mesh):
    placed = (P("ci", None), P(None, "co", "ci"), P("co", "ci"))
    return jax.shard_map(
        body,
        mesh=mesh,
        in_specs=placed,
        out_specs=(P("co", "ci"), P("ci", "co"), P(None, "co", "ci")),
        check_vma=False,
    )
```

```python
import jax
import jax.numpy as jnp
from jax import lax
from jax.experimental import pallas as pl
from jax.experimental.pallas import tpu as pltpu
from jax.sharding import PartitionSpec as P


NY = 8
NZ = 8
AREA = NY * NZ
LANES = 128
F32 = jnp.float32
BF16 = jnp.bfloat16


VMEM = pltpu.VMEM
H_FLIP = 0
CI_FLIP = 7
Z_ORDER = (7, 6, 5, 4, 3, 2, 1, 0)
SHIFTS = [(b, c) for b in (-1, 0, 1) for c in (-1, 0, 1)]


def in_vmem(n):
    return [pl.BlockSpec(memory_space=VMEM)] * n


def shift_rows(value, b, c):
    rows, lanes = value.shape
    if c:
        z = lax.broadcasted_iota(jnp.int32, value.shape, 0) % NZ
        rolled = pltpu.roll(value, (-c) % rows, 0)
        value = jnp.where(z == (NZ - 1 if c > 0 else 0), 0.0, rolled)
    if b:
        cube = value.reshape(rows // AREA, NY, NZ, lanes)
        edge = jnp.zeros((rows // AREA, 1, NZ, lanes), value.dtype)
        if b > 0:
            cube = jnp.concatenate([cube[:, 1:], edge], axis=1)
        else:
            cube = jnp.concatenate([edge, cube[:, :-1]], axis=1)
        value = cube.reshape(rows, lanes)
    return value


def position():
    co = lax.axis_index("co")
    return lax.rem(co, 2), co // (lax.axis_size("co") // 2)


def flip(index, mask):
    return lax.bitwise_xor(index, mask)


def receiver():
    return lax.axis_index("ci")


def pack_kernel(grad_ref, out_ref):
    tiles = []
    for t in range(2):
        tile = grad_ref[:, t * LANES:(t + 1) * LANES].astype(F32)
        tiles += [tile, pltpu.roll(tile, AREA, 1)]
    packed = jnp.concatenate(tiles, axis=0).T[:AREA].astype(BF16)
    for r in range(out_ref.shape[0]):
        out_ref[r] = packed


def response_kernel(x_ref, f_ref, keep_ref, send_ref, wide_ref, lhs, rhs):
    groups = 2 * keep_ref.shape[0]
    planes = 4 * groups
    rows = groups * AREA
    width = 4 * LANES
    zero = jnp.zeros((AREA, LANES), BF16)
    rhs[192:, :] = jnp.zeros((AREA, 3 * width), BF16)
    for b in range(3):
        lhs[0:AREA, b * width:b * width + LANES] = zero
        lhs[2 * rows - AREA:2 * rows, (b + 1) * width - LANES:(b + 1) * width] = zero
        for c in range(3):
            for i in range(2):
                for j in range(4):
                    a = j - 1 - i
                    block = f_ref[(a + 1) * 9 + b * 3 + c] if -1 <= a <= 1 else jnp.zeros((32, LANES), BF16)
                    rhs[c * 64 + i * 32:c * 64 + (i + 1) * 32, b * width + j * LANES:b * width + (j + 1) * LANES] = block
    for pair in range(planes // 2):
        cells = x_ref[:, pair * LANES:(pair + 1) * LANES].astype(F32).T
        for b in range(3):
            moved = shift_rows(cells, b - 1, 0).astype(BF16)
            for i in range(2):
                piece = moved[i * AREA:(i + 1) * AREA]
                spots = [(pair, i + 1)]
                if i == 1 and pair + 1 < planes // 2:
                    spots.append((pair + 1, 0))
                if i == 0 and pair:
                    spots.append((pair - 1, 3))
                for p, j in spots:
                    at = (p % 2) * rows + (p // 2) * AREA
                    lhs[at:at + AREA, b * width + j * LANES:b * width + (j + 1) * LANES] = piece
    wide_ref[...] = lhs[:, width:2 * width]
    lane = lax.broadcasted_iota(jnp.int32, (rows, LANES), 1)
    parts = []
    for half in range(2):
        full = lax.dot_general(
            lhs[half * rows:(half + 1) * rows, :], rhs[...], (((1,), (1,)), ((), ())), preferred_element_type=F32
        )
        first = full[:, :LANES]
        last = full[:, LANES:]
        sides = shift_rows(first, 0, -1) + shift_rows(last, 0, 1)
        parts.append((sides, first))
    low = parts[0][0] + pltpu.roll(parts[0][1], AREA, 1)
    high = pltpu.roll(parts[1][0], AREA, 1) + parts[1][1]
    total = jnp.where(lane < AREA, low, high)
    mask = lax.bitwise_and(receiver(), groups // 2 - 1)
    lower = receiver() < groups // 2
    for g in range(groups // 2):
        near = total[g * AREA:(g + 1) * AREA]
        far = total[(g + groups // 2) * AREA:(g + groups // 2 + 1) * AREA]
        at = lax.bitwise_xor(mask, g)
        keep_ref[at] = jnp.where(lower, near, far)
        send_ref[at] = jnp.where(lower, far, near)


def add_kernel(mine_ref, other_ref, keep_ref, send_ref):
    for p in range(mine_ref.shape[0]):
        total = mine_ref[p] + other_ref[p]
        if p % 2:
            send_ref[p // 2] = total
        else:
            keep_ref[p // 2] = total


def response_out_kernel(mine_ref, other_ref, out_ref):
    total = mine_ref[0] + other_ref[0]
    turned = jnp.concatenate([total, total], axis=0).T
    lane = lax.broadcasted_iota(jnp.int32, (32, LANES), 1)
    for t in range(2):
        low = turned[t * 64:t * 64 + 32]
        high = turned[t * 64 + 32:t * 64 + 64]
        out_ref[:, t * LANES:(t + 1) * LANES] = jnp.where(lane < AREA, low, high).astype(BF16)


def in_grad_kernel(mine_ref, other_ref, f0_ref, f1_ref, f2_ref, f3_ref, out_ref, lhs, rhs):
    groups = out_ref.shape[0]
    held = groups // 2
    core, half = position()
    filters = (f0_ref, f1_ref, f2_ref, f3_ref)
    lane = lax.broadcasted_iota(jnp.int32, (AREA, LANES), 1)
    for source in range(4):
        ref = mine_ref if source < 2 else other_ref
        sel = half if source % 2 == 0 else 1 - half
        blocks = []
        for m in range(-1, held + 1):
            at = half * held + m
            block = ref[flip(sel, H_FLIP), flip(jnp.clip(at, 0, groups - 1), CI_FLIP)].astype(F32)
            if m in (-1, held):
                block = jnp.where(jnp.logical_and(at >= 0, at < groups), block, 0.0)
            blocks.append(block)
        early = [pltpu.roll(block, 32 * (1 - core), 1) for block in blocks[:-1]]
        late = [pltpu.roll(block, LANES - 32 * (core + 1), 1) for block in blocks[1:]]
        rows = []
        for m in range(held):
            rows.append(jnp.where(lane >= 32 * (1 - core), early[m + 1], early[m]))
            rows.append(jnp.where(lane < LANES - 32 * (core + 1), late[m], late[m + 1]))
        near = jnp.concatenate(rows, axis=0)
        for b in range(3):
            at = (b * 4 + source) * LANES
            lhs[:, at:at + LANES] = shift_rows(near, 1 - b, 0).astype(BF16)
            for c in range(3):
                for j in range(3):
                    rhs[at + j * 32:at + (j + 1) * 32, c * LANES:(c + 1) * LANES] = filters[source][(2 - j) * 9 + b * 3 + c]
                rhs[at + 96:at + LANES, c * LANES:(c + 1) * LANES] = jnp.zeros((32, LANES), BF16)
    full = jnp.dot(lhs[...], rhs[...], preferred_element_type=F32)
    total = shift_rows(full[:, :LANES], 0, 1) + full[:, LANES:2 * LANES] + shift_rows(full[:, 2 * LANES:], 0, -1)
    for k, z in enumerate(Z_ORDER):
        out_ref[k] = total[z * AREA:(z + 1) * AREA]


def filter_grad_kernel(mine_ref, wide_ref, out_ref, *, scale):
    groups = mine_ref.shape[1]
    rows = groups * AREA
    half = flip(position()[1], H_FLIP)
    cells = jnp.concatenate([mine_ref[half, k ^ CI_FLIP].astype(F32) for k in range(groups)], axis=0)
    turned = jnp.concatenate([cells[k * LANES:(k + 1) * LANES].T for k in range(rows // LANES)], axis=1)
    turned = jnp.concatenate([turned[:64], turned[64:]], axis=1)
    cells = turned.shape[1]
    index = lax.broadcasted_iota(jnp.int32, turned.shape, 1)
    z = index % NZ
    y = (index // NZ) % NY
    wide = wide_ref[...]
    for s, (b, c) in enumerate(SHIFTS):
        moved = turned
        step = b * NZ + c
        if step:
            moved = pltpu.roll(turned, step % cells, 1)
        if c:
            moved = jnp.where(z == (0 if c > 0 else NZ - 1), 0.0, moved)
        if b:
            moved = jnp.where(y == (0 if b > 0 else NY - 1), 0.0, moved)
        full = jnp.dot(moved.astype(BF16), wide, preferred_element_type=F32)
        for a in (-1, 0, 1):
            total = full[:32, (a + 1) * LANES:(a + 2) * LANES] + full[32:, (a + 2) * LANES:(a + 3) * LANES]
            out_ref[(a + 1) * 9 + s] = total * scale


LIMIT = 20 * 2**20


def params():
    return pltpu.CompilerParams(vmem_limit_bytes=LIMIT)


def cost(flops, moved):
    return pl.CostEstimate(flops=flops, transcendentals=0, bytes_accessed=moved)


def pack(out_grad, receivers):
    return pl.pallas_call(
        pack_kernel,
        out_shape=jax.ShapeDtypeStruct((receivers, AREA, LANES), BF16),
        in_specs=in_vmem(1),
        out_specs=in_vmem(1)[0],
        compiler_params=params(),
        name="pack",
    )(out_grad)


def response_terms(features, bank):
    groups = features.shape[1] // (4 * AREA)
    rows = groups * AREA
    return pl.pallas_call(
        response_kernel,
        out_shape=(
            jax.ShapeDtypeStruct((groups // 2, AREA, LANES), F32),
            jax.ShapeDtypeStruct((groups // 2, AREA, LANES), F32),
            jax.ShapeDtypeStruct((2 * rows, 4 * LANES), BF16),
        ),
        in_specs=in_vmem(2),
        out_specs=tuple(in_vmem(3)),
        scratch_shapes=[VMEM((2 * rows, 12 * LANES), BF16), VMEM((2 * LANES, 12 * LANES), BF16)],
        compiler_params=params(),
        cost_estimate=cost(2 * 27 * 32 * 128 * 2048, 2 * 10**6),
        name="response_terms",
    )(features, bank)


def add_terms(mine, other):
    part = jax.ShapeDtypeStruct((mine.shape[0] // 2, AREA, LANES), F32)
    return pl.pallas_call(
        add_kernel,
        out_shape=(part, part),
        in_specs=in_vmem(2),
        out_specs=tuple(in_vmem(2)),
        compiler_params=params(),
        name="add_terms",
    )(mine, other)


def response_out(mine, other):
    return pl.pallas_call(
        response_out_kernel,
        out_shape=jax.ShapeDtypeStruct((32, 4 * AREA), BF16),
        in_specs=in_vmem(2),
        out_specs=in_vmem(1)[0],
        compiler_params=params(),
        name="response_out",
    )(mine, other)


def in_grad_terms(mine, other, banks):
    groups = mine.shape[1]
    rows = groups * AREA
    return pl.pallas_call(
        in_grad_kernel,
        out_shape=jax.ShapeDtypeStruct((groups, AREA, LANES), F32),
        in_specs=in_vmem(6),
        out_specs=in_vmem(1)[0],
        scratch_shapes=[VMEM((rows, 12 * LANES), BF16), VMEM((12 * LANES, 3 * LANES), BF16)],
        compiler_params=params(),
        cost_estimate=cost(2 * 27 * 32 * 128 * 2048, 2 * 10**6),
        name="in_grad_terms",
    )(mine, other, *banks)


def filter_terms(mine, wide, scale):
    return pl.pallas_call(
        lambda *refs: filter_grad_kernel(*refs, scale=scale),
        out_shape=jax.ShapeDtypeStruct((27, 32, LANES), F32),
        in_specs=in_vmem(2),
        out_specs=in_vmem(1)[0],
        compiler_params=params(),
        cost_estimate=cost(2 * 27 * 32 * 128 * 2048, 2 * 10**6),
        name="filter_terms",
    )(mine, wide)


def body(features, bank, out_grad):
    cell_count = features.shape[1]
    n_ci = lax.axis_size("ci")
    n_co = lax.axis_size("co")
    column = n_co // 2
    other_y = [(i, (i + column) % n_co) for i in range(n_co)]
    other_core = [(i, i ^ 1) for i in range(n_co)]
    gather_groups = [
        [((h ^ H_FLIP) * column + k) * n_ci + (i ^ CI_FLIP) for h in range(2) for i in range(n_ci)] for k in range(column)
    ]
    sum_groups = [[h * column + 2 * z + c for z in Z_ORDER] for h in range(2) for c in range(2)]
    flips = [[(i, i ^ d) for i in range(n_ci)] for d in (n_ci // 2, 1, 2)]
    packed = pack(out_grad, 2 * n_ci)
    mine = lax.all_to_all(packed, ("co", "ci"), 0, 0, tiled=True, axis_index_groups=gather_groups)
    mine = mine.reshape(2, n_ci, AREA, LANES)
    bank_y = lax.ppermute(bank, "co", other_y)
    bank_c = lax.ppermute(bank, "co", other_core)
    bank_cy = lax.ppermute(bank_y, "co", other_core)
    keep, send, wide = response_terms(features, bank)
    came = lax.ppermute(send, "ci", flips[0])
    keep, send = add_terms(keep, came)
    came = lax.ppermute(send, "ci", flips[1])
    keep, send = add_terms(keep, came)
    came = lax.ppermute(send, "ci", flips[2])
    response = response_out(keep, came)
    other = lax.ppermute(mine, "co", other_core)
    shares = in_grad_terms(mine, other, (bank, bank_y, bank_c, bank_cy))
    shares = lax.all_to_all(shares, "co", 0, 0, tiled=True, axis_index_groups=sum_groups)
    in_grad = jnp.sum(shares, axis=0).T.astype(BF16)
    filter_grad = filter_terms(mine, wide, float(cell_count) ** (-0.5))
    return (response, in_grad, filter_grad)


def solution(mesh):
    placed = (P("ci", None), P(None, "co", "ci"), P("co", "ci"))
    return jax.shard_map(
        body,
        mesh=mesh,
        in_specs=placed,
        out_specs=(P("co", "ci"), P("ci", "co"), P(None, "co", "ci")),
        check_vma=False,
    )
```

```python
import jax
import jax.numpy as jnp
from jax import lax
from jax.experimental import pallas as pl
from jax.experimental.pallas import tpu as pltpu
from jax.sharding import PartitionSpec as P


NY = 8
NZ = 8
AREA = NY * NZ
LANES = 128
F32 = jnp.float32
BF16 = jnp.bfloat16


VMEM = pltpu.VMEM
H_FLIP = 0
CI_FLIP = 7
Z_ORDER = (6, 5, 4, 3, 2, 1, 0, 7)
SHIFTS = [(b, c) for b in (-1, 0, 1) for c in (-1, 0, 1)]


def in_vmem(n):
    return [pl.BlockSpec(memory_space=VMEM)] * n


def shift_rows(value, b, c):
    rows, lanes = value.shape
    if c:
        z = lax.broadcasted_iota(jnp.int32, value.shape, 0) % NZ
        rolled = pltpu.roll(value, (-c) % rows, 0)
        value = jnp.where(z == (NZ - 1 if c > 0 else 0), 0.0, rolled)
    if b:
        cube = value.reshape(rows // AREA, NY, NZ, lanes)
        edge = jnp.zeros((rows // AREA, 1, NZ, lanes), value.dtype)
        if b > 0:
            cube = jnp.concatenate([cube[:, 1:], edge], axis=1)
        else:
            cube = jnp.concatenate([edge, cube[:, :-1]], axis=1)
        value = cube.reshape(rows, lanes)
    return value


def position():
    co = lax.axis_index("co")
    return lax.rem(co, 2), co // (lax.axis_size("co") // 2)


def flip(index, mask):
    return lax.bitwise_xor(index, mask)


def receiver():
    return lax.axis_index("ci")


def pack_kernel(grad_ref, out_ref):
    tiles = []
    for t in range(2):
        tile = grad_ref[:, t * LANES:(t + 1) * LANES].astype(F32)
        tiles += [tile, pltpu.roll(tile, AREA, 1)]
    packed = jnp.concatenate(tiles, axis=0).T[:AREA].astype(BF16)
    for r in range(out_ref.shape[0]):
        out_ref[r] = packed


def response_kernel(x_ref, f_ref, keep_ref, send_ref, wide_ref, lhs, rhs):
    groups = 2 * keep_ref.shape[0]
    planes = 4 * groups
    rows = groups * AREA
    width = 4 * LANES
    zero = jnp.zeros((AREA, LANES), BF16)
    rhs[192:, :] = jnp.zeros((AREA, 3 * width), BF16)
    for b in range(3):
        lhs[0:AREA, b * width:b * width + LANES] = zero
        lhs[2 * rows - AREA:2 * rows, (b + 1) * width - LANES:(b + 1) * width] = zero
        for c in range(3):
            for i in range(2):
                for j in range(4):
                    a = j - 1 - i
                    block = f_ref[(a + 1) * 9 + b * 3 + c] if -1 <= a <= 1 else jnp.zeros((32, LANES), BF16)
                    rhs[c * 64 + i * 32:c * 64 + (i + 1) * 32, b * width + j * LANES:b * width + (j + 1) * LANES] = block
    for pair in range(planes // 2):
        cells = x_ref[:, pair * LANES:(pair + 1) * LANES].astype(F32).T
        for b in range(3):
            moved = shift_rows(cells, b - 1, 0).astype(BF16)
            for i in range(2):
                piece = moved[i * AREA:(i + 1) * AREA]
                spots = [(pair, i + 1)]
                if i == 1 and pair + 1 < planes // 2:
                    spots.append((pair + 1, 0))
                if i == 0 and pair:
                    spots.append((pair - 1, 3))
                for p, j in spots:
                    at = (p % 2) * rows + (p // 2) * AREA
                    lhs[at:at + AREA, b * width + j * LANES:b * width + (j + 1) * LANES] = piece
    wide_ref[...] = lhs[:, width:2 * width]
    lane = lax.broadcasted_iota(jnp.int32, (rows, LANES), 1)
    parts = []
    for half in range(2):
        full = lax.dot_general(
            lhs[half * rows:(half + 1) * rows, :], rhs[...], (((1,), (1,)), ((), ())), preferred_element_type=F32
        )
        first = full[:, :LANES]
        last = full[:, LANES:]
        sides = shift_rows(first, 0, -1) + shift_rows(last, 0, 1)
        parts.append((sides, first))
    low = parts[0][0] + pltpu.roll(parts[0][1], AREA, 1)
    high = pltpu.roll(parts[1][0], AREA, 1) + parts[1][1]
    total = jnp.where(lane < AREA, low, high)
    mask = lax.bitwise_and(receiver(), groups // 2 - 1)
    lower = receiver() < groups // 2
    for g in range(groups // 2):
        near = total[g * AREA:(g + 1) * AREA]
        far = total[(g + groups // 2) * AREA:(g + groups // 2 + 1) * AREA]
        at = lax.bitwise_xor(mask, g)
        keep_ref[at] = jnp.where(lower, near, far)
        send_ref[at] = jnp.where(lower, far, near)


def add_kernel(mine_ref, other_ref, keep_ref, send_ref):
    for p in range(mine_ref.shape[0]):
        total = mine_ref[p] + other_ref[p]
        if p % 2:
            send_ref[p // 2] = total
        else:
            keep_ref[p // 2] = total


def response_out_kernel(mine_ref, other_ref, out_ref):
    total = mine_ref[0] + other_ref[0]
    turned = jnp.concatenate([total, total], axis=0).T
    lane = lax.broadcasted_iota(jnp.int32, (32, LANES), 1)
    for t in range(2):
        low = turned[t * 64:t * 64 + 32]
        high = turned[t * 64 + 32:t * 64 + 64]
        out_ref[:, t * LANES:(t + 1) * LANES] = jnp.where(lane < AREA, low, high).astype(BF16)


def in_grad_kernel(grad_ref, near_ref, far_ref, *rest):
    *start, out_ref, lhs, rhs = rest
    groups = out_ref.shape[0]
    held = groups // 2
    core, half = position()
    lane = lax.broadcasted_iota(jnp.int32, (AREA, LANES), 1)
    for source, bank_ref in enumerate((near_ref, far_ref)):
        sel = half if source == 0 else 1 - half
        blocks = []
        for m in range(-1, held + 1):
            at = half * held + m
            block = grad_ref[flip(sel, H_FLIP), flip(jnp.clip(at, 0, groups - 1), CI_FLIP)].astype(F32)
            if m in (-1, held):
                block = jnp.where(jnp.logical_and(at >= 0, at < groups), block, 0.0)
            blocks.append(block)
        early = [pltpu.roll(block, 32 * (1 - core), 1) for block in blocks[:-1]]
        late = [pltpu.roll(block, LANES - 32 * (core + 1), 1) for block in blocks[1:]]
        rows = []
        for m in range(held):
            rows.append(jnp.where(lane >= 32 * (1 - core), early[m + 1], early[m]))
            rows.append(jnp.where(lane < LANES - 32 * (core + 1), late[m], late[m + 1]))
        near = jnp.concatenate(rows, axis=0)
        for b in range(3):
            at = (b * 2 + source) * LANES
            lhs[:, at:at + LANES] = shift_rows(near, 1 - b, 0).astype(BF16)
            for c in range(3):
                for j in range(3):
                    rhs[at + j * 32:at + (j + 1) * 32, c * LANES:(c + 1) * LANES] = bank_ref[(2 - j) * 9 + b * 3 + c]
                rhs[at + 96:at + LANES, c * LANES:(c + 1) * LANES] = jnp.zeros((32, LANES), BF16)
    full = jnp.dot(lhs[...], rhs[...], preferred_element_type=F32)
    total = shift_rows(full[:, :LANES], 0, 1) + full[:, LANES:2 * LANES] + shift_rows(full[:, 2 * LANES:], 0, -1)
    for k, z in enumerate(Z_ORDER):
        part = total[z * AREA:(z + 1) * AREA]
        out_ref[k] = part + start[0][k] if start else part


def filter_grad_kernel(mine_ref, wide_ref, out_ref, *, scale):
    groups = mine_ref.shape[1]
    rows = groups * AREA
    half = flip(position()[1], H_FLIP)
    cells = jnp.concatenate([mine_ref[half, k ^ CI_FLIP].astype(F32) for k in range(groups)], axis=0)
    turned = jnp.concatenate([cells[k * LANES:(k + 1) * LANES].T for k in range(rows // LANES)], axis=1)
    turned = jnp.concatenate([turned[:64], turned[64:]], axis=1)
    cells = turned.shape[1]
    index = lax.broadcasted_iota(jnp.int32, turned.shape, 1)
    z = index % NZ
    y = (index // NZ) % NY
    wide = wide_ref[...]
    for s, (b, c) in enumerate(SHIFTS):
        moved = turned
        step = b * NZ + c
        if step:
            moved = pltpu.roll(turned, step % cells, 1)
        if c:
            moved = jnp.where(z == (0 if c > 0 else NZ - 1), 0.0, moved)
        if b:
            moved = jnp.where(y == (0 if b > 0 else NY - 1), 0.0, moved)
        full = jnp.dot(moved.astype(BF16), wide, preferred_element_type=F32)
        for a in (-1, 0, 1):
            total = full[:32, (a + 1) * LANES:(a + 2) * LANES] + full[32:, (a + 2) * LANES:(a + 3) * LANES]
            out_ref[(a + 1) * 9 + s] = total * scale


LIMIT = 20 * 2**20


def params():
    return pltpu.CompilerParams(vmem_limit_bytes=LIMIT)


def cost(flops, moved):
    return pl.CostEstimate(flops=flops, transcendentals=0, bytes_accessed=moved)


def pack(out_grad, receivers):
    return pl.pallas_call(
        pack_kernel,
        out_shape=jax.ShapeDtypeStruct((receivers, AREA, LANES), BF16),
        in_specs=in_vmem(1),
        out_specs=in_vmem(1)[0],
        compiler_params=params(),
        name="pack",
    )(out_grad)


def response_terms(features, bank):
    groups = features.shape[1] // (4 * AREA)
    rows = groups * AREA
    return pl.pallas_call(
        response_kernel,
        out_shape=(
            jax.ShapeDtypeStruct((groups // 2, AREA, LANES), F32),
            jax.ShapeDtypeStruct((groups // 2, AREA, LANES), F32),
            jax.ShapeDtypeStruct((2 * rows, 4 * LANES), BF16),
        ),
        in_specs=in_vmem(2),
        out_specs=tuple(in_vmem(3)),
        scratch_shapes=[VMEM((2 * rows, 12 * LANES), BF16), VMEM((2 * LANES, 12 * LANES), BF16)],
        compiler_params=params(),
        cost_estimate=cost(2 * 27 * 32 * 128 * 2048, 2 * 10**6),
        name="response_terms",
    )(features, bank)


def add_terms(mine, other):
    part = jax.ShapeDtypeStruct((mine.shape[0] // 2, AREA, LANES), F32)
    return pl.pallas_call(
        add_kernel,
        out_shape=(part, part),
        in_specs=in_vmem(2),
        out_specs=tuple(in_vmem(2)),
        compiler_params=params(),
        name="add_terms",
    )(mine, other)


def response_out(mine, other):
    return pl.pallas_call(
        response_out_kernel,
        out_shape=jax.ShapeDtypeStruct((32, 4 * AREA), BF16),
        in_specs=in_vmem(2),
        out_specs=in_vmem(1)[0],
        compiler_params=params(),
        name="response_out",
    )(mine, other)


def in_grad_terms(grads, banks, *start):
    groups = grads.shape[1]
    rows = groups * AREA
    return pl.pallas_call(
        in_grad_kernel,
        out_shape=jax.ShapeDtypeStruct((groups, AREA, LANES), F32),
        in_specs=in_vmem(3 + len(start)),
        out_specs=in_vmem(1)[0],
        scratch_shapes=[VMEM((rows, 6 * LANES), BF16), VMEM((6 * LANES, 3 * LANES), BF16)],
        compiler_params=params(),
        cost_estimate=cost(27 * 32 * 128 * 2048, 10**6),
        name="in_grad_terms",
    )(grads, *banks, *start)


def filter_terms(mine, wide, scale):
    return pl.pallas_call(
        lambda *refs: filter_grad_kernel(*refs, scale=scale),
        out_shape=jax.ShapeDtypeStruct((27, 32, LANES), F32),
        in_specs=in_vmem(2),
        out_specs=in_vmem(1)[0],
        compiler_params=params(),
        cost_estimate=cost(2 * 27 * 32 * 128 * 2048, 2 * 10**6),
        name="filter_terms",
    )(mine, wide)


def body(features, bank, out_grad):
    cell_count = features.shape[1]
    n_ci = lax.axis_size("ci")
    n_co = lax.axis_size("co")
    column = n_co // 2
    other_y = [(i, (i + column) % n_co) for i in range(n_co)]
    other_core = [(i, i ^ 1) for i in range(n_co)]
    gather_groups = [
        [((h ^ H_FLIP) * column + k) * n_ci + (i ^ CI_FLIP) for h in range(2) for i in range(n_ci)] for k in range(column)
    ]
    sum_groups = [[h * column + 2 * z + c for z in Z_ORDER] for h in range(2) for c in range(2)]
    flips = [[(i, i ^ d) for i in range(n_ci)] for d in (n_ci // 2, 1, 2)]
    packed = pack(out_grad, 2 * n_ci)
    mine = lax.all_to_all(packed, ("co", "ci"), 0, 0, tiled=True, axis_index_groups=gather_groups)
    mine = mine.reshape(2, n_ci, AREA, LANES)
    bank_y = lax.ppermute(bank, "co", other_y)
    bank_c = lax.ppermute(bank, "co", other_core)
    bank_cy = lax.ppermute(bank_y, "co", other_core)
    keep, send, wide = response_terms(features, bank)
    came = lax.ppermute(send, "ci", flips[0])
    keep, send = add_terms(keep, came)
    came = lax.ppermute(send, "ci", flips[1])
    keep, send = add_terms(keep, came)
    came = lax.ppermute(send, "ci", flips[2])
    response = response_out(keep, came)
    other = lax.ppermute(mine, "co", other_core)
    shares = in_grad_terms(mine, (bank, bank_y))
    shares = in_grad_terms(other, (bank_c, bank_cy), shares)
    shares = lax.all_to_all(shares, "co", 0, 0, tiled=True, axis_index_groups=sum_groups)
    in_grad = jnp.sum(shares, axis=0).T.astype(BF16)
    filter_grad = filter_terms(mine, wide, float(cell_count) ** (-0.5))
    return (response, in_grad, filter_grad)


def solution(mesh):
    placed = (P("ci", None), P(None, "co", "ci"), P("co", "ci"))
    return jax.shard_map(
        body,
        mesh=mesh,
        in_specs=placed,
        out_specs=(P("co", "ci"), P("ci", "co"), P(None, "co", "ci")),
        check_vma=False,
    )
```
